32 devices in a mesh: slab: 8 (over z, y), mode: 4 (over x, core).
Axes of the slice: x: 2, y: 2, z: 4, core: 2. Of those that a mesh axis runs over, the one named last changes fastest.
Arguments:
- eigvec: bfloat16 [10240, 3, 1024], P('slab', None, 'mode'), may hold values from -6 to 6
- species: int32 [10240], P('slab'), may hold values from 0 to 3
- mode_cot: float32 [1024], P('mode'), may hold values from -4 to 4
- neighbours: int32 [10240, 16], P('slab'), may hold values from 0 to 2560, as said below
- pair_features: bfloat16 [163840, 128], P(('slab', 'mode')), may hold values from -130 to 130
- w_in: bfloat16 [128, 256], replicated, may hold values from -0.5 to 0.5
- b_in: float32 [256], replicated, may hold values from -3 to 3
- w_out: bfloat16 [9, 256], replicated, may hold values from -0.375 to 0.375
Outputs:
- features_grad: bfloat16 [163840, 128], P(('slab', 'mode'))
- grad_w_in: float32 [128, 256], replicated
- grad_b_in: float32 [256], replicated
- grad_w_out: float32 [9, 256], replicated
The draws below stay inside these ranges and needn't reach their ends.
Inputs may be any that keep to these rules, and one draw needn't show every extreme that they name: `neighbours`: atom r of a slab (0 to 1279) lists extended indices from r to r + 1280; extended index x stands for atom (slab * 1280 + x - 640) mod 10240; the value 1280 + 2 * 640 marks an empty slot.
All inputs are finite; a program needn't handle non-finite values.
Results may differ from the reference program's by a relative error of at most 0.019.
Values may be sent and summed in bfloat16 or wider, within the bound.
A program may use at most 64 MiB of HBM per device.

```python
import math
import jax
import jax.numpy as jnp
from jax import lax

A_DEV = 1280
RIM = 640
NBR = 16
MODES = 1024
F = 128
H = 256
ATOMS = 10240
PAIRS = 163840
N_SLAB = 8


def draw_neighbours(key, part):
    first_key, second_key = jax.random.split(key)
    local = jnp.arange(ATOMS, dtype=jnp.int32) % A_DEV
    slot = jnp.arange(NBR, dtype=jnp.int32)
    offset = jax.random.randint(first_key, (ATOMS, NBR), 0, 2 * RIM + 1)
    offset = jnp.where((local[:, None] == 0) & (slot[None, :] == 0), 0, offset)
    counts = jax.random.randint(second_key, (ATOMS,), 10, NBR + 1)
    counts = jnp.where(local == 0, 10, counts)
    live_slot = slot[None, :] < counts[:, None]
    return jnp.where(live_slot, local[:, None] + offset, A_DEV + 2 * RIM).astype(jnp.int32)


def draw_pair_features(key, part):
    col_key, base_key = jax.random.split(key, 2)
    column_scale = jnp.exp(jax.random.uniform(col_key, (F,), minval=0.0, maxval=math.log(10.0)))
    ramp = 1.0 + 2.0 * jnp.arange(PAIRS, dtype=jnp.float32) / PAIRS
    base = jnp.clip(jax.random.normal(base_key, (PAIRS, F)), -4.0, 4.0)
    return (base * ramp[:, None] * column_scale[None, :]).astype(jnp.bfloat16)


def with_ends(drawn, rng, low, high):
    longest = drawn.shape.index(max(drawn.shape))
    spots = []
    for shift in (0, 1):
        where = [jax.random.randint(jax.random.fold_in(rng, axis), (), 0, length) for axis, length in enumerate(drawn.shape)]
        where[longest] = (where[longest] + shift) % drawn.shape[longest]
        spots.append(tuple(where))
    return drawn.at[spots[0]].set(low).at[spots[1]].set(high)


def block_scale(own_key, shape, shards, low, high):
    gain = 1.0
    for position, parts in shards:
        heights = jax.random.uniform(jax.random.fold_in(jax.random.fold_in(own_key, 6), position), (parts,), jnp.float32, low / len(shards), high / len(shards))
        gain = gain * jnp.repeat(jnp.exp(heights), shape[position] // parts).reshape((-1,) + (1,) * (len(shape) - 1 - position))
    return gain


def centred(rng, dims, width, limit, shards=(), kind=jnp.bfloat16):
    values = width * jax.random.normal(rng, dims, jnp.float32)
    if shards:
        values = values * block_scale(rng, dims, shards, -0.22, 0.18)
    return jnp.clip(values, -limit, limit).astype(kind)


def setup_inputs(seed: int = 0) -> dict:
    keys = jax.random.split(jax.random.key(seed), 9)
    return {
        "eigvec": centred(keys[0], (ATOMS, 3, MODES), 1.0, 6.0, ((0, 8), (2, 4))),
        "species": with_ends(jax.random.randint(keys[1], (ATOMS,), 0, 4), jax.random.fold_in(keys[1], 1), 0, 3).astype(jnp.int32),
        "mode_cot": centred(keys[2], (MODES,), 1.0, 4.0, ((0, 4),), jnp.float32),
        "neighbours": draw_neighbours(jax.random.fold_in(keys[8], 71), 0),
        "pair_features": draw_pair_features(jax.random.fold_in(keys[8], 71), 0),
        "w_in": centred(keys[5], (F, H), F ** -0.5, 0.5),
        "b_in": centred(keys[6], (H,), 0.5, 3.0, (), jnp.float32),
        "w_out": centred(keys[7], (9, H), H ** -0.5, 0.375),
    }


MASS_TABLE = (1.35, 2.94, 2.79, 2.95)
CLIP_NORM = 100.0

def atom_masses(species):
    kinds = jnp.arange(4, dtype=jnp.int32)
    onehot = (species[:, None] == kinds[None, :]).astype(jnp.float32)
    return lax.optimization_barrier(jnp.sum(onehot * jnp.asarray(MASS_TABLE, jnp.float32)[None, :], axis=1))

def mlp_backward(features, pair_cot, w_in, b_in, w_out):
    preact = jnp.dot(features, w_in, preferred_element_type=jnp.float32) + b_in[None, :]
    sigmoid_pre = jax.nn.sigmoid(preact)
    hidden = (preact * sigmoid_pre).astype(jnp.bfloat16)
    hidden_cot = lax.dot_general(pair_cot, w_out, (((0,), (0,)), ((), ())), preferred_element_type=jnp.float32)
    pre_cot = (hidden_cot * sigmoid_pre * (1.0 + preact * (1.0 - sigmoid_pre))).astype(jnp.bfloat16)
    features_grad = lax.dot_general(pre_cot, w_in, (((1,), (1,)), ((), ())), preferred_element_type=jnp.float32).astype(jnp.bfloat16)
    grad_w_in = lax.dot_general(features, pre_cot, (((0,), (0,)), ((), ())), preferred_element_type=jnp.float32)
    grad_b_in = lax.optimization_barrier(jnp.sum(pre_cot.astype(jnp.float32), axis=0))
    grad_w_out = jnp.dot(pair_cot, hidden, preferred_element_type=jnp.float32)
    return (features_grad, grad_w_in, grad_b_in, grad_w_out)

def reference(eigvec, species, mode_cot, neighbours, pair_features, w_in, b_in, w_out):
    inv_root = lax.rsqrt(atom_masses(species))
    scaled = (eigvec.astype(jnp.float32) * inv_root[:, None, None]).astype(jnp.bfloat16)
    weighted = (scaled.astype(jnp.float32) * mode_cot[None, None, :]).astype(jnp.bfloat16)
    sentinel = A_DEV + 2 * RIM

    def per_slab(carry, slab_index):
        first_row = slab_index * A_DEV
        weighted_rows = lax.dynamic_slice_in_dim(weighted, first_row, A_DEV, 0).astype(jnp.float32)
        own_rows = lax.dynamic_slice_in_dim(scaled, first_row, A_DEV, 0).astype(jnp.float32)
        nbr_rows = lax.dynamic_slice_in_dim(neighbours, first_row, A_DEV, 0)
        live_mask = nbr_rows < sentinel
        partner_index = jnp.where(live_mask, (first_row + nbr_rows - RIM) % ATOMS, 0).astype(jnp.int32)
        partners = jnp.take(scaled, partner_index.reshape(-1), axis=0).reshape(A_DEV, NBR, 3, MODES).astype(jnp.float32)
        pair_terms = jnp.einsum('iam,ikbm->abik', weighted_rows, partners, precision=lax.Precision.HIGHEST).reshape(9, A_DEV, NBR)
        self_terms = jnp.einsum('iam,ibm->abi', weighted_rows, own_rows, precision=lax.Precision.HIGHEST).reshape(9, A_DEV)
        pair_cot = ((pair_terms - self_terms[:, :, None]) * live_mask[None].astype(jnp.float32)).astype(jnp.bfloat16)
        pair_cot = pair_cot.reshape(9, A_DEV * NBR)
        features = lax.dynamic_slice_in_dim(pair_features, first_row * NBR, A_DEV * NBR, 0)
        features_grad, part_w_in, part_b_in, part_w_out = mlp_backward(features, pair_cot, w_in, b_in, w_out)
        return ((carry[0] + part_w_in, carry[1] + part_b_in, carry[2] + part_w_out), features_grad)
    start = (jnp.zeros((F, H), jnp.float32), jnp.zeros((H,), jnp.float32), jnp.zeros((9, H), jnp.float32))
    sums, grads = lax.scan(per_slab, start, jnp.arange(N_SLAB, dtype=jnp.int32))
    raw_w_in, raw_b_in, raw_w_out = sums
    norm_sq = jnp.sum(raw_w_in * raw_w_in) + jnp.sum(raw_b_in * raw_b_in) + jnp.sum(raw_w_out * raw_w_out)
    factor = jnp.minimum(1.0, CLIP_NORM / jnp.sqrt(norm_sq + 1e-06))
    return (grads.reshape(PAIRS, F), raw_w_in * factor, raw_b_in * factor, raw_w_out * factor)
```

```python
import functools
import math

import jax
import jax.numpy as jnp
from jax import lax
from jax.experimental import pallas as pl
from jax.experimental.pallas import tpu as pltpu
from jax.sharding import PartitionSpec as P

MASS_TABLE = (1.35, 2.94, 2.79, 2.95)
CLIP_NORM = 100.0
TILE = 128
VMEM_LIMIT = 62 * 1024 * 1024
MESH = pl.DeviceIdType.MESH
VMEM = pl.BlockSpec(memory_space=pltpu.VMEM)
ANY = pl.BlockSpec(memory_space=pl.ANY)


def rows_of(block):
    return pl.ds(pl.multiple_of(block * TILE, TILE), TILE)


def kernel(slabs, groups, eig_ref, species_ref, cot_ref, nbr_ref, x_hbm, w_in_ref, b_in_ref, w_out_ref,
           grad_ref, everyone,
           eig, x_ref, species_row, w_rep_ref, panel, weighted, nbr_in, low_ref, high_ref, even, odd, firsts, lasts, outgoing,
           own_in, far_in, forward, returned, total_first, total_last, hidden_ref, slope_ref, pre_ref,
           w_out_sum, sums, sums_out, near_in, mine, rounds, summed,
           eig_sem, x_sem, rim_send, rim_recv, nbr_send, nbr_recv, pair_send, own_recv, far_recv,
           forward_send, returned_recv, near_send, near_recv, slab_send, slab_recv, back_send, back_recv):
    slab, mode = lax.axis_index("slab"), lax.axis_index("mode")
    atoms = eig.shape[1]
    slot_count = nbr_ref.shape[0]
    blocks = atoms // TILE
    rim = blocks // 2
    eights = TILE // 8
    sentinel = 2 * atoms
    share = atoms // groups
    fold = 8 * TILE // slot_count
    features = x_ref.shape[1]
    quarter = mine.shape[0]

    def blocks_of(owner):
        return list(range(owner * share // TILE, -(-(owner + 1) * share // TILE)))

    width = max(len(blocks_of(owner)) for owner in range(groups))
    owned = {block: [(owner, blocks_of(owner).index(block)) for owner in range(groups) if block in blocks_of(owner)]
             for block in range(blocks)}

    def peer_mode(hop):
        return lax.rem(mode + hop, groups)

    def peer_slab(hop):
        return lax.rem(slab + hop, slabs)

    previous, following = peer_slab(slabs - 1), peer_slab(1)

    eig_copies = [pltpu.make_async_copy(
        eig_ref.at[:, block * TILE : (block + 1) * TILE, :], eig.at[:, block * TILE : (block + 1) * TILE, :],
        eig_sem.at[block]) for block in range(rim)]
    eig_copies.append(pltpu.make_async_copy(
        eig_ref.at[:, rim * TILE :, :], eig.at[:, rim * TILE :, :], eig_sem.at[rim]))
    for copy in eig_copies:
        copy.start()
    x_copy = pltpu.make_async_copy(x_hbm, x_ref, x_sem.at[0])
    x_copy.start()

    barrier = pltpu.get_barrier_semaphore()
    for hop in range(1, groups):
        pl.semaphore_signal(barrier, inc=1, device_id=(slab, peer_mode(hop)), device_id_type=MESH)

    def greet(hop, _):
        pl.semaphore_signal(barrier, inc=1, device_id=(peer_slab(hop), mode), device_id_type=MESH)
        return 0

    lax.fori_loop(1, slabs, greet, 0)
    species_row[...] = species_ref[...].reshape(species_row.shape)
    roots = [1.0 / math.sqrt(mass) for mass in MASS_TABLE]

    def scale(block):
        kinds = jnp.transpose(jnp.broadcast_to(
            species_row[:, rows_of(block)], (TILE, TILE)))
        root = jnp.full((TILE, TILE), roots[0], jnp.float32)
        for kind in range(1, len(roots)):
            root = jnp.where(kinds == kind, roots[kind], root)
        root = jnp.concatenate([root] * (eig.shape[2] // TILE), axis=1)
        for a in range(3):
            panel[a, rows_of(block), :] = (eig[a, rows_of(block), :].astype(jnp.float32) * root).astype(jnp.bfloat16)

    def weigh(block):
        for a in range(3):
            weighted[a, rows_of(block), :] = (
                panel[a, rows_of(block), :].astype(jnp.float32) * cot_ref[...]).astype(jnp.bfloat16)

    def tables(slots, base, block):
        spread = jnp.transpose(jnp.concatenate([slots] * (TILE // slot_count), axis=0))
        offset = spread - base * TILE
        low_ref[rows_of(block), :] = offset & (TILE - 1)
        high_ref[rows_of(block), :] = lax.shift_right_arithmetic(offset, 7)

    rim_copies = [pltpu.make_async_remote_copy(
        src_ref=panel.at[:, q * TILE : (q + 1) * TILE, :],
        dst_ref=panel.at[:, (blocks + q) * TILE : (blocks + q + 1) * TILE, :],
        send_sem=rim_send.at[q], recv_sem=rim_recv.at[q],
        device_id=(previous, mode), device_id_type=MESH) for q in range(rim)]
    nbr_copy = pltpu.make_async_remote_copy(
        src_ref=nbr_ref.at[:, 0 : rim * TILE], dst_ref=nbr_in, send_sem=nbr_send.at[0], recv_sem=nbr_recv.at[0],
        device_id=(previous, mode), device_id_type=MESH)

    eig_copies[0].wait()
    scale(0)
    pl.semaphore_wait(barrier, groups - 1 + slabs - 1)
    rim_copies[0].start()
    nbr_copy.start()
    for q in range(1, rim):
        eig_copies[q].wait()
        scale(q)
        rim_copies[q].start()
    eig_copies[rim].wait()

    def begin(block, _):
        scale(block)
        return 0

    lax.fori_loop(rim, blocks, begin, 0)

    def ready(block, _):
        weigh(block)
        tables(nbr_ref[:, rows_of(block)], block, block)
        return 0

    lax.fori_loop(0, blocks, ready, 0)

    prods = (even, odd)

    def product(buffer, tile, left_block, right_block):
        left = jnp.concatenate([weighted[a, rows_of(left_block), :] for a in range(3)], axis=0)
        right = jnp.concatenate([panel[b, rows_of(right_block), :] for b in range(3)], axis=0)
        prods[buffer][tile] = lax.dot_general(
            left, right, (((1,), (1,)), ((), ())), preferred_element_type=jnp.float32)

    position = lax.broadcasted_iota(jnp.int32, (8, TILE), 1) // slot_count

    def pick(buffer, eight, block, entries, diagonal):
        rows = pl.ds(pl.multiple_of(block * TILE + 8 * eight, 8), 8)
        lane, high = low_ref[rows, :], high_ref[rows, :]
        hits = [high == distance for _, distance in entries]
        first = jnp.zeros((8, TILE), jnp.float32)
        if diagonal is not None:
            live = (high * TILE + lane + block * TILE) < sentinel
            same = lax.broadcasted_iota(jnp.int32, (8, TILE), 0) + 8 * eight
        for part in range(9):
            a, b = part // 3, part % 3
            piece = pl.ds(pl.multiple_of(a * TILE + 8 * eight, 8), 8)
            picked = jnp.zeros((8, TILE), jnp.float32)
            for (tile, _), hit in zip(entries, hits):
                values = prods[buffer][tile, piece, b * TILE : (b + 1) * TILE]
                picked = jnp.where(
                    hit, jnp.take_along_axis(values, lane, axis=1, mode="promise_in_bounds"), picked)
            if diagonal is not None:
                values = prods[buffer][diagonal, piece, b * TILE : (b + 1) * TILE]
                own = jnp.take_along_axis(values, same, axis=1, mode="promise_in_bounds")
                picked = jnp.where(live, picked - own, 0.0)
            if part < 8:
                first = jnp.where(position == part, picked, first)
        return rows, first, picked

    tiles = 3 * rim + 1
    assert tiles == eights

    def own_product(pair, tile):
        second = (tile + 2 * rim - pair) // tiles
        product(pair % 2, tile, pair + rim * second, tile - (rim + 1) * second)

    def own_pick(pair, eight):
        for block, entries, diagonal in (
            (pair, [(t, t - pair + rim) for t in range(rim + 1 + pair)], pair),
            (pair + rim, [(rim + 1 + pair + t, t) for t in range(2 * rim - pair)], 2 * rim + 1 + pair),
        ):
            rows, first, last = pick(pair % 2, eight, block, entries, diagonal)
            firsts[rows, :] = first
            lasts[rows, :] = last

    def lead(tile, _):
        own_product(0, tile)
        return 0

    lax.fori_loop(0, tiles, lead, 0)
    for pair in range(rim):
        def own_step(step, _):
            for half in range(2):
                own_pick(pair, 2 * step + half)
                if pair + 1 < rim:
                    own_product(pair + 1, 2 * step + half)
            return 0

        lax.fori_loop(0, tiles // 2, own_step, 0)

    def pack(block):
        outgoing[block, 0:TILE, :] = firsts[rows_of(block), :].astype(jnp.bfloat16)
        folds = []
        for unit in range(TILE // fold):
            folded = jnp.zeros((8, TILE), jnp.float32)
            for p in range(fold // 8):
                folded = jnp.where(
                    position == p, lasts[pl.ds(block * TILE + unit * fold + 8 * p, 8), :], folded)
            folds.append(folded)
        outgoing[block, TILE:, :] = jnp.concatenate(folds, axis=0).astype(jnp.bfloat16)

    def pair_copy(block, index, owner, place, hop):
        target, sems = (own_in, own_recv) if block < blocks else (far_in, far_recv)
        return pltpu.make_async_remote_copy(
            src_ref=outgoing.at[block], dst_ref=target.at[hop, place], send_sem=pair_send.at[block, index],
            recv_sem=sems.at[hop, place], device_id=(slab, owner), device_id_type=MESH)

    def deliver(block, action):
        for index, (owner, place) in enumerate(owned[block % blocks]):
            @pl.when(mode != owner)
            def _():
                copy = pair_copy(block, index, owner, place, lax.rem(mode - owner + groups, groups) - 1)
                if action == "start":
                    copy.start()
                else:
                    copy.wait_send()

    for block in range(rim):
        pack(block)
        deliver(block, "start")

    for part in range(8):
        w_rep_ref[part * slot_count : (part + 1) * slot_count, :] = jnp.broadcast_to(
            w_out_ref[part : part + 1, :].astype(jnp.float32), (slot_count, w_rep_ref.shape[1])).astype(jnp.bfloat16)
    w_rep_ref[TILE:, :] = jnp.broadcast_to(
        w_out_ref[8:9, :].astype(jnp.float32), (TILE, w_rep_ref.shape[1])).astype(jnp.bfloat16)
    x_copy.wait()
    unit_rows = fold * slot_count
    units = share // fold

    def before(unit, _):
        here = pl.ds(pl.multiple_of(unit * unit_rows, unit_rows), unit_rows)
        preact = jnp.dot(x_ref[here, :], w_in_ref[...], preferred_element_type=jnp.float32) + b_in_ref[...]
        gate = jax.nn.sigmoid(preact)
        hidden_ref[here, :] = (preact * gate).astype(jnp.bfloat16)
        slope_ref[here, :] = gate * (1.0 + preact * (1.0 - gate))
        return 0

    lax.fori_loop(0, units, before, 0)
    sums[...] = jnp.zeros_like(sums)
    w_out_sum[...] = jnp.zeros_like(w_out_sum)

    nbr_copy.wait_recv()

    def foreign(q, _):
        tables(nbr_in[:, rows_of(q)], q, blocks + q)
        return 0

    lax.fori_loop(0, rim, foreign, 0)

    def relay(q):
        for owner, place in owned[q]:
            @pl.when(mode == owner)
            def _():
                total = outgoing[blocks + q].astype(jnp.float32)
                for hop in range(groups - 1):
                    pair_copy(blocks + q, 0, owner, place, hop).wait_recv()
                    total = total + far_in[hop, place].astype(jnp.float32)
                forward[place] = total.astype(jnp.bfloat16)
                relay_copy(place).start()

    def relay_copy(place):
        return pltpu.make_async_remote_copy(
            src_ref=forward.at[place], dst_ref=returned.at[place], send_sem=forward_send.at[place],
            recv_sem=returned_recv.at[place], device_id=(following, mode), device_id_type=MESH)

    for q in range(rim):
        rim_copies[q].wait_recv()
        weigh(blocks + q)

        def rim_product(tile, _):
            second = (tile + 1 + q) // (rim + 1)
            product(0, tile, blocks + q - rim * second, rim + q + tile)
            return 0

        lax.fori_loop(0, rim + 1, rim_product, 0)

        def rim_pick(eight, _):
            for part in range(4):
                rows, first, last = pick(0, 4 * eight + part, blocks + q, [(t, t) for t in range(rim - q)], None)
                firsts[rows, :] = first
                lasts[rows, :] = last
            for part in range(4):
                rows, first, last = pick(
                    0, 4 * eight + part, rim + q, [(rim - q + t, 2 * rim + t - q) for t in range(q + 1)], None)
                firsts[rows, :] += first
                lasts[rows, :] += last
            return 0

        lax.fori_loop(0, eights // 4, rim_pick, 0)
        pack(blocks + q)
        deliver(blocks + q, "start")
        pack(rim + q)
        deliver(rim + q, "start")
        if q:
            relay(q - 1)

    base = mode * share // TILE
    first_unit = mode * share // fold - base * (TILE // fold)

    def gather_block(place):
        total = outgoing[base + place].astype(jnp.float32)
        for hop in range(groups - 1):
            pltpu.make_async_remote_copy(
                src_ref=outgoing.at[0], dst_ref=own_in.at[hop, place], send_sem=pair_send.at[0, 0],
                recv_sem=own_recv.at[hop, place], device_id=(slab, peer_mode(1)), device_id_type=MESH).wait_recv()
            total = total + own_in[hop, place].astype(jnp.float32)
        total_first[place * TILE : (place + 1) * TILE, :] = total[0:TILE]
        total_last[place * (TILE // 8) * slot_count // 16 : (place + 1) * (TILE // 8) * slot_count // 16, :] = total[TILE:]

        @pl.when(mode < groups // 2)
        def _():
            relay_copy(place).wait_recv()
            more = returned[place].astype(jnp.float32)
            total_first[place * TILE : (place + 1) * TILE, :] += more[0:TILE]
            total_last[place * (TILE // 8) * slot_count // 16 : (place + 1) * (TILE // 8) * slot_count // 16, :] += more[TILE:]

    row = lax.broadcasted_iota(jnp.int32, (unit_rows, TILE), 0)
    lane = lax.broadcasted_iota(jnp.int32, (unit_rows, TILE), 1)

    def expand(block, mask):
        wide = jnp.broadcast_to(block[:, None, :], (fold, slot_count, TILE)).reshape(unit_rows, TILE)
        return jnp.where(mask, wide, 0.0).astype(jnp.bfloat16)

    def after(unit, _):
        keep = lax.rem(row, slot_count) == lax.rem(lane, slot_count)
        keep_last = keep & (row // (8 * slot_count) == lane // slot_count)
        here = pl.ds(pl.multiple_of(unit * unit_rows, unit_rows), unit_rows)
        first = total_first[pl.ds(pl.multiple_of((unit + first_unit) * fold, fold), fold), :]
        last = total_last[pl.ds(pl.multiple_of((unit + first_unit) * 8, 8), 8), :]
        spread = jnp.concatenate(
            [expand(first, keep), expand(jnp.concatenate([last] * (fold // 8), axis=0), keep_last)], axis=1)
        hidden_cot = jnp.dot(spread, w_rep_ref[...], preferred_element_type=jnp.float32)
        pre_cot = (hidden_cot * slope_ref[here, :]).astype(jnp.bfloat16)
        pre_ref[here, :] = pre_cot
        sums[0:features, :] += lax.dot_general(
            x_ref[here, :], pre_cot, (((0,), (0,)), ((), ())), preferred_element_type=jnp.float32)
        sums[features : features + 1, :] += jnp.sum(pre_cot.astype(jnp.float32), axis=0, keepdims=True)
        w_out_sum[...] += lax.dot_general(
            spread, hidden_ref[here, :], (((0,), (0,)), ((), ())), preferred_element_type=jnp.float32)
        return 0

    early = (width - 1) * (TILE // fold) - 1
    for place in range(width - 1):
        gather_block(place)
    lax.fori_loop(0, early, after, 0)
    relay(rim - 1)
    gather_block(width - 1)
    lax.fori_loop(early, units, after, 0)
    for part in range(9):
        end = (part + 1) * slot_count if part < 8 else 2 * TILE
        sums[features + 1 + part : features + 2 + part, :] = jnp.sum(
            w_out_sum[part * slot_count : end, :], axis=0, keepdims=True)

    for group in range(groups):
        sums_out[group] = sums[group * quarter : (group + 1) * quarter, :].astype(jnp.bfloat16)
    near = [pltpu.make_async_remote_copy(
        src_ref=sums_out.at[peer_mode(hop)], dst_ref=near_in.at[hop - 1], send_sem=near_send.at[hop - 1],
        recv_sem=near_recv.at[hop - 1], device_id=(slab, peer_mode(hop)), device_id_type=MESH)
        for hop in range(1, groups)]
    for copy in near:
        copy.start()
    for copy in near:
        copy.wait_recv()
    total = sums[pl.ds(pl.multiple_of(mode * quarter, 8), quarter), :]
    for hop in range(1, groups):
        total = total + near_in[hop - 1].astype(jnp.float32)
    mine[...] = total.astype(jnp.bfloat16)

    def slab_copy(hop):
        return pltpu.make_async_remote_copy(
            src_ref=mine, dst_ref=rounds.at[slab], send_sem=slab_send.at[hop],
            recv_sem=slab_recv.at[slab], device_id=(peer_slab(hop), mode), device_id_type=MESH)

    def slab_copy_from(hop):
        return pltpu.make_async_remote_copy(
            src_ref=mine, dst_ref=rounds.at[peer_slab(hop)], send_sem=slab_send.at[hop],
            recv_sem=slab_recv.at[peer_slab(hop)], device_id=(peer_slab(hop), mode), device_id_type=MESH)

    def send(hop, _):
        slab_copy(hop).start()
        return 0

    def settle(hop, _):
        slab_copy_from(hop).wait_recv()
        return 0

    def sent(hop, _):
        slab_copy(hop).wait_send()
        return 0

    lax.fori_loop(1, slabs, send, 0)
    rounds[slab] = mine[...]

    def finish(unit, _):
        here = pl.ds(pl.multiple_of(unit * unit_rows, unit_rows), unit_rows)
        grad_ref[here, :] = lax.dot_general(
            pre_ref[here, :], w_in_ref[...], (((1,), (1,)), ((), ())), preferred_element_type=jnp.float32
        ).astype(jnp.bfloat16)
        return 0

    lax.fori_loop(0, units, finish, 0)
    lax.fori_loop(1, slabs, settle, 0)
    summed[...] = lax.fori_loop(
        1, slabs, lambda index, value: value + rounds[index].astype(jnp.float32), rounds[0].astype(jnp.float32)
    ).astype(jnp.bfloat16)
    back = [pltpu.make_async_remote_copy(
        src_ref=summed, dst_ref=everyone.at[mode], send_sem=back_send.at[hop - 1],
        recv_sem=back_recv.at[hop - 1], device_id=(slab, peer_mode(hop)), device_id_type=MESH)
        for hop in range(1, groups)]
    back_from = [pltpu.make_async_remote_copy(
        src_ref=summed, dst_ref=everyone.at[peer_mode(groups - hop)], send_sem=back_send.at[hop - 1],
        recv_sem=back_recv.at[hop - 1], device_id=(slab, peer_mode(hop)), device_id_type=MESH)
        for hop in range(1, groups)]
    for copy in back:
        copy.start()
    everyone[mode] = summed[...]

    for copy in rim_copies:
        copy.wait_send()
    nbr_copy.wait_send()
    for block in range(blocks + rim):
        deliver(block, "sent")

    @pl.when(mode < groups // 2)
    def _():
        for place in range(width):
            relay_copy(place).wait_send()

    for copy in near:
        copy.wait_send()
    lax.fori_loop(1, slabs, sent, 0)

    for copy in back_from:
        copy.wait_recv()
    for copy in back:
        copy.wait_send()


def clip_kernel(raw_ref, grad_ref, grad_hbm, w_in_out, b_in_out, w_out_out, grad_sem):
    copy = pltpu.make_async_copy(grad_ref, grad_hbm, grad_sem.at[0])
    copy.start()
    features = w_in_out.shape[0]
    raw = jnp.concatenate([raw_ref[group].astype(jnp.float32) for group in range(raw_ref.shape[0])], axis=0)
    factor = jnp.minimum(1.0, CLIP_NORM / jnp.sqrt(jnp.sum(raw * raw, keepdims=True) + 1e-6))
    scaled = raw * factor
    w_in_out[...] = scaled[0:features, :]
    b_in_out[...] = scaled[features : features + 1, :].reshape(b_in_out.shape)
    w_out_out[...] = scaled[features + 1 : features + 10, :]
    copy.wait()


def shards(slabs, groups, eigvec, species, mode_cot, neighbours, pair_features, w_in, b_in, w_out):
    atoms, _, modes = eigvec.shape
    slot_count = neighbours.shape[1]
    features, hidden_width = w_in.shape
    pairs = pair_features.shape[0]
    blocks = atoms // TILE
    rim = blocks // 2
    fold = 8 * TILE // slot_count
    share = atoms // groups
    width = max(-(-(owner + 1) * share // TILE) - owner * share // TILE for owner in range(groups))
    lasts = TILE * slot_count // TILE
    everything = blocks + rim
    quarter = -(-(features + 10) // (groups * 16)) * 16
    bf16, f32, i32 = jnp.bfloat16, jnp.float32, jnp.int32
    dma = pltpu.SemaphoreType.DMA
    grads, raw = pl.pallas_call(
        functools.partial(kernel, slabs, groups),
        out_shape=(
            jax.ShapeDtypeStruct(pair_features.shape, bf16),
            jax.ShapeDtypeStruct((groups, quarter, hidden_width), bf16),
        ),
        in_specs=[ANY, VMEM, VMEM, VMEM, ANY, VMEM, VMEM, VMEM],
        out_specs=(VMEM, VMEM),
        scratch_shapes=[
            pltpu.VMEM((3, atoms, modes), bf16),
            pltpu.VMEM(pair_features.shape, bf16),
            pltpu.VMEM((1, atoms), i32),
            pltpu.VMEM((2 * TILE, hidden_width), bf16),
            pltpu.VMEM((3, everything * TILE, modes), bf16),
            pltpu.VMEM((3, everything * TILE, modes), bf16),
            pltpu.VMEM((slot_count, rim * TILE), i32),
            pltpu.VMEM((everything * TILE, TILE), i32),
            pltpu.VMEM((everything * TILE, TILE), i32),
            pltpu.VMEM((3 * rim + 1, 3 * TILE, 3 * TILE), f32),
            pltpu.VMEM((3 * rim + 1, 3 * TILE, 3 * TILE), f32),
            pltpu.VMEM((everything * TILE, TILE), f32),
            pltpu.VMEM((everything * TILE, TILE), f32),
            pltpu.VMEM((everything, TILE + lasts, TILE), bf16),
            pltpu.VMEM((groups - 1, width, TILE + lasts, TILE), bf16),
            pltpu.VMEM((groups - 1, width, TILE + lasts, TILE), bf16),
            pltpu.VMEM((width, TILE + lasts, TILE), bf16),
            pltpu.VMEM((width, TILE + lasts, TILE), bf16),
            pltpu.VMEM((width * TILE, TILE), f32),
            pltpu.VMEM((width * lasts, TILE), f32),
            pltpu.VMEM((pairs, hidden_width), bf16),
            pltpu.VMEM((pairs, hidden_width), f32),
            pltpu.VMEM((pairs, hidden_width), bf16),
            pltpu.VMEM((2 * TILE, hidden_width), f32),
            pltpu.VMEM((groups * quarter, hidden_width), f32),
            pltpu.VMEM((groups, quarter, hidden_width), bf16),
            pltpu.VMEM((groups - 1, quarter, hidden_width), bf16),
            pltpu.VMEM((quarter, hidden_width), bf16),
            pltpu.VMEM((slabs, quarter, hidden_width), bf16),
            pltpu.VMEM((quarter, hidden_width), bf16),
            dma((rim + 1,)), dma((1,)), dma((rim,)), dma((rim,)), dma((1,)), dma((1,)),
            dma((everything, 2)), dma((groups - 1, width)), dma((groups - 1, width)),
            dma((width,)), dma((width,)),
            dma((groups - 1,)), dma((groups - 1,)), dma((slabs,)), dma((slabs,)),
            dma((groups - 1,)), dma((groups - 1,)),
        ],
        compiler_params=pltpu.CompilerParams(
            collective_id=0, has_side_effects=True, vmem_limit_bytes=VMEM_LIMIT),
        name="phonon",
    )(jnp.transpose(eigvec, (1, 0, 2)), species, mode_cot[None, :], neighbours.T, pair_features,
      w_in, b_in[None, :], w_out)
    return pl.pallas_call(
        clip_kernel,
        out_shape=(
            jax.ShapeDtypeStruct(pair_features.shape, bf16),
            jax.ShapeDtypeStruct((features, hidden_width), f32),
            jax.ShapeDtypeStruct((hidden_width,), f32),
            jax.ShapeDtypeStruct((9, hidden_width), f32),
        ),
        in_specs=[VMEM, VMEM],
        out_specs=(ANY, VMEM, VMEM, VMEM),
        scratch_shapes=[dma((1,))],
        compiler_params=pltpu.CompilerParams(vmem_limit_bytes=8 * 1024 * 1024),
        name="clip",
    )(raw, grads)


def solution(mesh):
    return jax.shard_map(
        functools.partial(shards, mesh.shape["slab"], mesh.shape["mode"]),
        mesh=mesh,
        in_specs=(
            P("slab", None, "mode"),
            P("slab"),
            P("mode"),
            P("slab", None),
            P(("slab", "mode"), None),
            P(),
            P(),
            P(),
        ),
        out_specs=(P(("slab", "mode"), None), P(), P(), P()),
        check_vma=False,
    )
```

```python
import functools
import math

import jax
import jax.numpy as jnp
from jax import lax
from jax.experimental import pallas as pl
from jax.experimental.pallas import tpu as pltpu
from jax.sharding import PartitionSpec as P

MASS_TABLE = (1.35, 2.94, 2.79, 2.95)
CLIP_NORM = 100.0
TILE = 128
VMEM_LIMIT = 62 * 1024 * 1024
MESH = pl.DeviceIdType.MESH
VMEM = pl.BlockSpec(memory_space=pltpu.VMEM)
ANY = pl.BlockSpec(memory_space=pl.ANY)
HBM = pl.BlockSpec(memory_space=pltpu.HBM)


def rows_of(block):
    return pl.ds(pl.multiple_of(block * TILE, TILE), TILE)


def kernel(slabs, groups, eig_ref, species_hbm, cot_hbm, nbr_hbm, x_hbm, w_in_hbm, b_in_hbm, w_out_hbm,
           grad_hbm, everyone,
           species_ref, cot_ref, nbr_ref, w_in_ref, b_in_ref, w_out_ref, eig, x_ref, species_row, w_rep_ref, panel, weighted, nbr_in, low_ref, high_ref, even, odd, firsts, lasts, outgoing,
           own_in, far_in, forward, returned, total_first, total_last, hidden_ref, slope_ref, pre_ref, grad_ref,
           w_out_sum, sums, sums_out, near_in, mine, rounds, summed,
           small_sem, eig_sem, x_sem, rim_send, rim_recv, nbr_send, nbr_recv, pair_send, own_recv, far_recv,
           forward_send, returned_recv, near_send, near_recv, slab_send, slab_recv, back_send, back_recv, grad_sem):
    slab, mode = lax.axis_index("slab"), lax.axis_index("mode")
    atoms = eig.shape[1]
    slot_count = nbr_ref.shape[0]
    blocks = atoms // TILE
    rim = blocks // 2
    eights = TILE // 8
    sentinel = 2 * atoms
    share = atoms // groups
    fold = 8 * TILE // slot_count
    features = x_ref.shape[1]
    quarter = mine.shape[0]

    def blocks_of(owner):
        return list(range(owner * share // TILE, -(-(owner + 1) * share // TILE)))

    width = max(len(blocks_of(owner)) for owner in range(groups))
    owned = {block: [(owner, blocks_of(owner).index(block)) for owner in range(groups) if block in blocks_of(owner)]
             for block in range(blocks)}

    def peer_mode(hop):
        return lax.rem(mode + hop, groups)

    def peer_slab(hop):
        return lax.rem(slab + hop, slabs)

    previous, following = peer_slab(slabs - 1), peer_slab(1)

    small = [pltpu.make_async_copy(source, target, small_sem.at[index]) for index, (source, target) in enumerate((
        (species_hbm, species_ref), (nbr_hbm, nbr_ref), (cot_hbm, cot_ref), (w_in_hbm, w_in_ref),
        (b_in_hbm, b_in_ref), (w_out_hbm, w_out_ref)))]
    small[0].start()
    eig_copies = [pltpu.make_async_copy(
        eig_ref.at[:, block * TILE : (block + 1) * TILE, :], eig.at[:, block * TILE : (block + 1) * TILE, :],
        eig_sem.at[block]) for block in range(rim)]
    eig_copies.append(pltpu.make_async_copy(
        eig_ref.at[:, rim * TILE :, :], eig.at[:, rim * TILE :, :], eig_sem.at[rim]))
    for copy in eig_copies[0:1] + small[1:] + eig_copies[1:]:
        copy.start()
    x_copy = pltpu.make_async_copy(x_hbm, x_ref, x_sem.at[0])
    x_copy.start()

    barrier = pltpu.get_barrier_semaphore()
    for hop in range(1, groups):
        pl.semaphore_signal(barrier, inc=1, device_id=(slab, peer_mode(hop)), device_id_type=MESH)

    def greet(hop, _):
        pl.semaphore_signal(barrier, inc=1, device_id=(peer_slab(hop), mode), device_id_type=MESH)
        return 0

    lax.fori_loop(1, slabs, greet, 0)
    small[0].wait()
    species_row[...] = species_ref[...].reshape(species_row.shape)
    roots = [1.0 / math.sqrt(mass) for mass in MASS_TABLE]

    def scale(block):
        kinds = jnp.transpose(jnp.broadcast_to(
            species_row[:, rows_of(block)], (TILE, TILE)))
        root = jnp.full((TILE, TILE), roots[0], jnp.float32)
        for kind in range(1, len(roots)):
            root = jnp.where(kinds == kind, roots[kind], root)
        root = jnp.concatenate([root] * (eig.shape[2] // TILE), axis=1)
        for a in range(3):
            panel[a, rows_of(block), :] = (eig[a, rows_of(block), :].astype(jnp.float32) * root).astype(jnp.bfloat16)

    def weigh(block):
        for a in range(3):
            weighted[a, rows_of(block), :] = (
                panel[a, rows_of(block), :].astype(jnp.float32) * cot_ref[...]).astype(jnp.bfloat16)

    def tables(slots, base, block):
        spread = jnp.transpose(jnp.concatenate([slots] * (TILE // slot_count), axis=0))
        offset = spread - base * TILE
        low_ref[rows_of(block), :] = offset & (TILE - 1)
        high_ref[rows_of(block), :] = lax.shift_right_arithmetic(offset, 7)

    rim_copies = [pltpu.make_async_remote_copy(
        src_ref=panel.at[:, q * TILE : (q + 1) * TILE, :],
        dst_ref=panel.at[:, (blocks + q) * TILE : (blocks + q + 1) * TILE, :],
        send_sem=rim_send.at[q], recv_sem=rim_recv.at[q],
        device_id=(previous, mode), device_id_type=MESH) for q in range(rim)]
    nbr_copy = pltpu.make_async_remote_copy(
        src_ref=nbr_ref.at[:, 0 : rim * TILE], dst_ref=nbr_in, send_sem=nbr_send.at[0], recv_sem=nbr_recv.at[0],
        device_id=(previous, mode), device_id_type=MESH)

    eig_copies[0].wait()
    scale(0)
    pl.semaphore_wait(barrier, groups - 1 + slabs - 1)
    rim_copies[0].start()
    small[1].wait()
    nbr_copy.start()
    for q in range(1, rim):
        eig_copies[q].wait()
        scale(q)
        rim_copies[q].start()
    eig_copies[rim].wait()
    small[2].wait()

    def begin(block, _):
        scale(block)
        return 0

    lax.fori_loop(rim, blocks, begin, 0)

    def ready(block, _):
        weigh(block)
        tables(nbr_ref[:, rows_of(block)], block, block)
        return 0

    lax.fori_loop(0, blocks, ready, 0)

    prods = (even, odd)

    def product(buffer, tile, left_block, right_block):
        left = jnp.concatenate([weighted[a, rows_of(left_block), :] for a in range(3)], axis=0)
        right = jnp.concatenate([panel[b, rows_of(right_block), :] for b in range(3)], axis=0)
        prods[buffer][tile] = lax.dot_general(
            left, right, (((1,), (1,)), ((), ())), preferred_element_type=jnp.float32)

    position = lax.broadcasted_iota(jnp.int32, (8, TILE), 1) // slot_count

    def pick(buffer, eight, block, entries, diagonal):
        rows = pl.ds(pl.multiple_of(block * TILE + 8 * eight, 8), 8)
        lane, high = low_ref[rows, :], high_ref[rows, :]
        hits = [high == distance for _, distance in entries]
        first = jnp.zeros((8, TILE), jnp.float32)
        if diagonal is not None:
            live = (high * TILE + lane + block * TILE) < sentinel
            same = lax.broadcasted_iota(jnp.int32, (8, TILE), 0) + 8 * eight
        for part in range(9):
            a, b = part // 3, part % 3
            piece = pl.ds(pl.multiple_of(a * TILE + 8 * eight, 8), 8)
            picked = jnp.zeros((8, TILE), jnp.float32)
            for (tile, _), hit in zip(entries, hits):
                values = prods[buffer][tile, piece, b * TILE : (b + 1) * TILE]
                picked = jnp.where(
                    hit, jnp.take_along_axis(values, lane, axis=1, mode="promise_in_bounds"), picked)
            if diagonal is not None:
                values = prods[buffer][diagonal, piece, b * TILE : (b + 1) * TILE]
                own = jnp.take_along_axis(values, same, axis=1, mode="promise_in_bounds")
                picked = jnp.where(live, picked - own, 0.0)
            if part < 8:
                first = jnp.where(position == part, picked, first)
        return rows, first, picked

    tiles = 3 * rim + 1
    assert tiles == eights

    def own_product(pair, tile):
        second = (tile + 2 * rim - pair) // tiles
        product(pair % 2, tile, pair + rim * second, tile - (rim + 1) * second)

    def own_pick(pair, eight):
        for block, entries, diagonal in (
            (pair, [(t, t - pair + rim) for t in range(rim + 1 + pair)], pair),
            (pair + rim, [(rim + 1 + pair + t, t) for t in range(2 * rim - pair)], 2 * rim + 1 + pair),
        ):
            rows, first, last = pick(pair % 2, eight, block, entries, diagonal)
            firsts[rows, :] = first
            lasts[rows, :] = last

    def lead(tile, _):
        own_product(0, 2 * tile)
        own_product(0, 2 * tile + 1)
        return 0

    lax.fori_loop(0, tiles // 2, lead, 0)
    for pair in range(rim):
        def own_step(step, _):
            for half in range(2):
                own_pick(pair, 2 * step + half)
                if pair + 1 < rim:
                    own_product(pair + 1, 2 * step + half)
            return 0

        lax.fori_loop(0, tiles // 2, own_step, 0)

    def pack(block):
        outgoing[block, 0:TILE, :] = firsts[rows_of(block), :].astype(jnp.bfloat16)
        folds = []
        for unit in range(TILE // fold):
            folded = jnp.zeros((8, TILE), jnp.float32)
            for p in range(fold // 8):
                folded = jnp.where(
                    position == p, lasts[pl.ds(block * TILE + unit * fold + 8 * p, 8), :], folded)
            folds.append(folded)
        outgoing[block, TILE:, :] = jnp.concatenate(folds, axis=0).astype(jnp.bfloat16)

    def pair_copy(block, index, owner, place, hop):
        target, sems = (own_in, own_recv) if block < blocks else (far_in, far_recv)
        return pltpu.make_async_remote_copy(
            src_ref=outgoing.at[block], dst_ref=target.at[hop, place], send_sem=pair_send.at[block, index],
            recv_sem=sems.at[hop, place], device_id=(slab, owner), device_id_type=MESH)

    def deliver(block, action):
        for index, (owner, place) in enumerate(owned[block % blocks]):
            @pl.when(mode != owner)
            def _():
                copy = pair_copy(block, index, owner, place, lax.rem(mode - owner + groups, groups) - 1)
                if action == "start":
                    copy.start()
                else:
                    copy.wait_send()

    for block in range(rim):
        pack(block)
        deliver(block, "start")

    for copy in small[3:]:
        copy.wait()
    for part in range(8):
        w_rep_ref[part * slot_count : (part + 1) * slot_count, :] = jnp.broadcast_to(
            w_out_ref[part : part + 1, :].astype(jnp.float32), (slot_count, w_rep_ref.shape[1])).astype(jnp.bfloat16)
    w_rep_ref[TILE:, :] = jnp.broadcast_to(
        w_out_ref[8:9, :].astype(jnp.float32), (TILE, w_rep_ref.shape[1])).astype(jnp.bfloat16)
    x_copy.wait()
    unit_rows = fold * slot_count
    units = share // fold

    def before(unit, _):
        here = pl.ds(pl.multiple_of(unit * unit_rows, unit_rows), unit_rows)
        preact = jnp.dot(x_ref[here, :], w_in_ref[...], preferred_element_type=jnp.float32) + b_in_ref[...]
        gate = jax.nn.sigmoid(preact)
        hidden_ref[here, :] = (preact * gate).astype(jnp.bfloat16)
        slope_ref[here, :] = gate * (1.0 + preact * (1.0 - gate))
        return 0

    lax.fori_loop(0, units, before, 0)
    sums[...] = jnp.zeros_like(sums)
    w_out_sum[...] = jnp.zeros_like(w_out_sum)

    nbr_copy.wait_recv()

    def foreign(q, _):
        tables(nbr_in[:, rows_of(q)], q, blocks + q)
        return 0

    lax.fori_loop(0, rim, foreign, 0)

    def relay(q):
        for owner, place in owned[q]:
            @pl.when(mode == owner)
            def _():
                total = outgoing[blocks + q].astype(jnp.float32)
                for hop in range(groups - 1):
                    pair_copy(blocks + q, 0, owner, place, hop).wait_recv()
                    total = total + far_in[hop, place].astype(jnp.float32)
                forward[place] = total.astype(jnp.bfloat16)
                relay_copy(place).start()

    def relay_copy(place):
        return pltpu.make_async_remote_copy(
            src_ref=forward.at[place], dst_ref=returned.at[place], send_sem=forward_send.at[place],
            recv_sem=returned_recv.at[place], device_id=(following, mode), device_id_type=MESH)

    for q in range(rim):
        rim_copies[q].wait_recv()
        weigh(blocks + q)

        def rim_product(step, _):
            for half in range(2):
                tile = 2 * step + half
                second = (tile + 1 + q) // (rim + 1)
                product(0, tile, blocks + q - rim * second, rim + q + tile)
            return 0

        lax.fori_loop(0, (rim + 1) // 2, rim_product, 0)

        def rim_pick(eight, _):
            for part in range(4):
                rows, first, last = pick(0, 4 * eight + part, blocks + q, [(t, t) for t in range(rim - q)], None)
                firsts[rows, :] = first
                lasts[rows, :] = last
            for part in range(4):
                rows, first, last = pick(
                    0, 4 * eight + part, rim + q, [(rim - q + t, 2 * rim + t - q) for t in range(q + 1)], None)
                firsts[rows, :] += first
                lasts[rows, :] += last
            return 0

        lax.fori_loop(0, eights // 4, rim_pick, 0)
        pack(blocks + q)
        deliver(blocks + q, "start")
        pack(rim + q)
        deliver(rim + q, "start")
        if q:
            relay(q - 1)

    base = mode * share // TILE
    first_unit = mode * share // fold - base * (TILE // fold)

    def gather_block(place):
        total = outgoing[base + place].astype(jnp.float32)
        for hop in range(groups - 1):
            pltpu.make_async_remote_copy(
                src_ref=outgoing.at[0], dst_ref=own_in.at[hop, place], send_sem=pair_send.at[0, 0],
                recv_sem=own_recv.at[hop, place], device_id=(slab, peer_mode(1)), device_id_type=MESH).wait_recv()
            total = total + own_in[hop, place].astype(jnp.float32)
        total_first[place * TILE : (place + 1) * TILE, :] = total[0:TILE]
        total_last[place * (TILE // 8) * slot_count // 16 : (place + 1) * (TILE // 8) * slot_count // 16, :] = total[TILE:]

        @pl.when(mode < groups // 2)
        def _():
            relay_copy(place).wait_recv()
            more = returned[place].astype(jnp.float32)
            total_first[place * TILE : (place + 1) * TILE, :] += more[0:TILE]
            total_last[place * (TILE // 8) * slot_count // 16 : (place + 1) * (TILE // 8) * slot_count // 16, :] += more[TILE:]

    keep = (lax.broadcasted_iota(jnp.int32, (slot_count, TILE), 0)
            == lax.rem(lax.broadcasted_iota(jnp.int32, (slot_count, TILE), 1), slot_count))

    def expand(block):
        wide = jnp.broadcast_to(block[:, None, :], (fold, slot_count, TILE))
        return jnp.where(keep[None], wide, 0.0).reshape(unit_rows, TILE).astype(jnp.bfloat16)

    def after(unit, _):
        here = pl.ds(pl.multiple_of(unit * unit_rows, unit_rows), unit_rows)
        first = total_first[pl.ds(pl.multiple_of((unit + first_unit) * fold, fold), fold), :]
        last = total_last[pl.ds(pl.multiple_of((unit + first_unit) * 8, 8), 8), :]
        last = jnp.concatenate([jnp.where(position == p, last, 0.0) for p in range(fold // 8)], axis=0)
        spread = jnp.concatenate([expand(first), expand(last)], axis=1)
        hidden_cot = jnp.dot(spread, w_rep_ref[...], preferred_element_type=jnp.float32)
        pre_cot = (hidden_cot * slope_ref[here, :]).astype(jnp.bfloat16)
        pre_ref[here, :] = pre_cot
        sums[0:features, :] += lax.dot_general(
            x_ref[here, :], pre_cot, (((0,), (0,)), ((), ())), preferred_element_type=jnp.float32)
        sums[features : features + 1, :] += jnp.sum(pre_cot.astype(jnp.float32), axis=0, keepdims=True)
        w_out_sum[...] += lax.dot_general(
            spread, hidden_ref[here, :], (((0,), (0,)), ((), ())), preferred_element_type=jnp.float32)
        return 0

    early = (width - 1) * (TILE // fold) - 1
    for place in range(width - 1):
        gather_block(place)
    lax.fori_loop(0, early - 1, after, 0)
    relay(rim - 1)
    lax.fori_loop(early - 1, early, after, 0)
    gather_block(width - 1)
    lax.fori_loop(early, units, after, 0)
    for part in range(9):
        end = (part + 1) * slot_count if part < 8 else 2 * TILE
        sums[features + 1 + part : features + 2 + part, :] = jnp.sum(
            w_out_sum[part * slot_count : end, :], axis=0, keepdims=True)

    for group in range(groups):
        sums_out[group] = sums[group * quarter : (group + 1) * quarter, :].astype(jnp.bfloat16)
    near = [pltpu.make_async_remote_copy(
        src_ref=sums_out.at[peer_mode(hop)], dst_ref=near_in.at[hop - 1], send_sem=near_send.at[hop - 1],
        recv_sem=near_recv.at[hop - 1], device_id=(slab, peer_mode(hop)), device_id_type=MESH)
        for hop in range(1, groups)]
    for copy in near:
        copy.start()
    for copy in near:
        copy.wait_recv()
    total = sums[pl.ds(pl.multiple_of(mode * quarter, 8), quarter), :]
    for hop in range(1, groups):
        total = total + near_in[hop - 1].astype(jnp.float32)
    mine[...] = total.astype(jnp.bfloat16)

    def slab_copy(hop):
        return pltpu.make_async_remote_copy(
            src_ref=mine, dst_ref=rounds.at[slab], send_sem=slab_send.at[hop],
            recv_sem=slab_recv.at[slab], device_id=(peer_slab(hop), mode), device_id_type=MESH)

    def slab_copy_from(hop):
        return pltpu.make_async_remote_copy(
            src_ref=mine, dst_ref=rounds.at[peer_slab(hop)], send_sem=slab_send.at[hop],
            recv_sem=slab_recv.at[peer_slab(hop)], device_id=(peer_slab(hop), mode), device_id_type=MESH)

    def send(hop, _):
        slab_copy(hop).start()
        return 0

    def settle(hop, _):
        slab_copy_from(hop).wait_recv()
        return 0

    def sent(hop, _):
        slab_copy(hop).wait_send()
        return 0

    lax.fori_loop(1, slabs, send, 0)
    rounds[slab] = mine[...]

    def grad_copy(unit):
        here = pl.ds(pl.multiple_of(unit * unit_rows, unit_rows), unit_rows)
        return pltpu.make_async_copy(grad_ref.at[here, :], grad_hbm.at[here, :], grad_sem.at[unit])

    def finish(unit, _):
        here = pl.ds(pl.multiple_of(unit * unit_rows, unit_rows), unit_rows)
        grad_ref[here, :] = lax.dot_general(
            pre_ref[here, :], w_in_ref[...], (((1,), (1,)), ((), ())), preferred_element_type=jnp.float32
        ).astype(jnp.bfloat16)
        grad_copy(unit).start()
        return 0

    lax.fori_loop(0, units, finish, 0)
    lax.fori_loop(1, slabs, settle, 0)
    summed[...] = lax.fori_loop(
        1, slabs, lambda index, value: value + rounds[index].astype(jnp.float32), rounds[0].astype(jnp.float32)
    ).astype(jnp.bfloat16)
    back = [pltpu.make_async_remote_copy(
        src_ref=summed, dst_ref=everyone.at[mode], send_sem=back_send.at[hop - 1],
        recv_sem=back_recv.at[hop - 1], device_id=(slab, peer_mode(hop)), device_id_type=MESH)
        for hop in range(1, groups)]
    back_from = [pltpu.make_async_remote_copy(
        src_ref=summed, dst_ref=everyone.at[peer_mode(groups - hop)], send_sem=back_send.at[hop - 1],
        recv_sem=back_recv.at[hop - 1], device_id=(slab, peer_mode(hop)), device_id_type=MESH)
        for hop in range(1, groups)]
    for copy in back:
        copy.start()
    everyone[mode] = summed[...]

    for copy in rim_copies:
        copy.wait_send()
    nbr_copy.wait_send()
    for block in range(blocks + rim):
        deliver(block, "sent")

    @pl.when(mode < groups // 2)
    def _():
        for place in range(width):
            relay_copy(place).wait_send()

    for copy in near:
        copy.wait_send()
    lax.fori_loop(1, slabs, sent, 0)

    def placed(unit, _):
        grad_copy(unit).wait()
        return 0

    lax.fori_loop(0, units, placed, 0)
    for copy in back_from:
        copy.wait_recv()
    for copy in back:
        copy.wait_send()


def clip_kernel(raw_ref, grad_in, grad_hbm, w_in_out, b_in_out, w_out_out, held, in_sem, out_sem):
    pieces = in_sem.shape[0]
    rows = held.shape[0] // pieces
    incoming, outgoing = [], []
    for piece in range(pieces):
        here = pl.ds(piece * rows, rows)
        incoming.append(pltpu.make_async_copy(grad_in.at[here, :], held.at[here, :], in_sem.at[piece]))
        outgoing.append(pltpu.make_async_copy(held.at[here, :], grad_hbm.at[here, :], out_sem.at[piece]))
        incoming[piece].start()
    for coming, going in zip(incoming, outgoing):
        coming.wait()
        going.start()
    features = w_in_out.shape[0]
    raw = jnp.concatenate([raw_ref[group].astype(jnp.float32) for group in range(raw_ref.shape[0])], axis=0)
    factor = jnp.minimum(1.0, CLIP_NORM / jnp.sqrt(jnp.sum(raw * raw, keepdims=True) + 1e-6))
    scaled = raw * factor
    w_in_out[...] = scaled[0:features, :]
    b_in_out[...] = scaled[features : features + 1, :].reshape(b_in_out.shape)
    w_out_out[...] = scaled[features + 1 : features + 10, :]
    for copy in outgoing:
        copy.wait()


def shards(slabs, groups, eigvec, species, mode_cot, neighbours, pair_features, w_in, b_in, w_out):
    atoms, _, modes = eigvec.shape
    slot_count = neighbours.shape[1]
    features, hidden_width = w_in.shape
    pairs = pair_features.shape[0]
    blocks = atoms // TILE
    rim = blocks // 2
    fold = 8 * TILE // slot_count
    share = atoms // groups
    width = max(-(-(owner + 1) * share // TILE) - owner * share // TILE for owner in range(groups))
    lasts = TILE * slot_count // TILE
    everything = blocks + rim
    quarter = -(-(features + 10) // (groups * 16)) * 16
    bf16, f32, i32 = jnp.bfloat16, jnp.float32, jnp.int32
    dma = pltpu.SemaphoreType.DMA
    grads, raw = pl.pallas_call(
        functools.partial(kernel, slabs, groups),
        out_shape=(
            jax.ShapeDtypeStruct(pair_features.shape, bf16),
            jax.ShapeDtypeStruct((groups, quarter, hidden_width), bf16),
        ),
        in_specs=[HBM] * 8,
        out_specs=(ANY, VMEM),
        scratch_shapes=[
            pltpu.VMEM(species.shape, i32),
            pltpu.VMEM((1, modes), f32),
            pltpu.VMEM((slot_count, atoms), i32),
            pltpu.VMEM(w_in.shape, bf16),
            pltpu.VMEM((1, hidden_width), f32),
            pltpu.VMEM(w_out.shape, bf16),
            pltpu.VMEM((3, atoms, modes), bf16),
            pltpu.VMEM(pair_features.shape, bf16),
            pltpu.VMEM((1, atoms), i32),
            pltpu.VMEM((2 * TILE, hidden_width), bf16),
            pltpu.VMEM((3, everything * TILE, modes), bf16),
            pltpu.VMEM((3, everything * TILE, modes), bf16),
            pltpu.VMEM((slot_count, rim * TILE), i32),
            pltpu.VMEM((everything * TILE, TILE), i32),
            pltpu.VMEM((everything * TILE, TILE), i32),
            pltpu.VMEM((3 * rim + 1, 3 * TILE, 3 * TILE), f32),
            pltpu.VMEM((3 * rim + 1, 3 * TILE, 3 * TILE), f32),
            pltpu.VMEM((everything * TILE, TILE), f32),
            pltpu.VMEM((everything * TILE, TILE), f32),
            pltpu.VMEM((everything, TILE + lasts, TILE), bf16),
            pltpu.VMEM((groups - 1, width, TILE + lasts, TILE), bf16),
            pltpu.VMEM((groups - 1, width, TILE + lasts, TILE), bf16),
            pltpu.VMEM((width, TILE + lasts, TILE), bf16),
            pltpu.VMEM((width, TILE + lasts, TILE), bf16),
            pltpu.VMEM((width * TILE, TILE), f32),
            pltpu.VMEM((width * lasts, TILE), f32),
            pltpu.VMEM((pairs, hidden_width), bf16),
            pltpu.VMEM((pairs, hidden_width), f32),
            pltpu.VMEM((pairs, hidden_width), bf16),
            pltpu.VMEM(pair_features.shape, bf16),
            pltpu.VMEM((2 * TILE, hidden_width), f32),
            pltpu.VMEM((groups * quarter, hidden_width), f32),
            pltpu.VMEM((groups, quarter, hidden_width), bf16),
            pltpu.VMEM((groups - 1, quarter, hidden_width), bf16),
            pltpu.VMEM((quarter, hidden_width), bf16),
            pltpu.VMEM((slabs, quarter, hidden_width), bf16),
            pltpu.VMEM((quarter, hidden_width), bf16),
            dma((6,)), dma((rim + 1,)), dma((1,)), dma((rim,)), dma((rim,)), dma((1,)), dma((1,)),
            dma((everything, 2)), dma((groups - 1, width)), dma((groups - 1, width)),
            dma((width,)), dma((width,)),
            dma((groups - 1,)), dma((groups - 1,)), dma((slabs,)), dma((slabs,)),
            dma((groups - 1,)), dma((groups - 1,)), dma((share // fold,)),
        ],
        compiler_params=pltpu.CompilerParams(
            collective_id=0, has_side_effects=True, vmem_limit_bytes=VMEM_LIMIT),
        name="phonon",
    )(jnp.transpose(eigvec, (1, 0, 2)), species, mode_cot[None, :], neighbours.T, pair_features,
      w_in, b_in[None, :], w_out)
    return pl.pallas_call(
        clip_kernel,
        out_shape=(
            jax.ShapeDtypeStruct(pair_features.shape, bf16),
            jax.ShapeDtypeStruct((features, hidden_width), f32),
            jax.ShapeDtypeStruct((hidden_width,), f32),
            jax.ShapeDtypeStruct((9, hidden_width), f32),
        ),
        in_specs=[VMEM, ANY],
        out_specs=(ANY, VMEM, VMEM, VMEM),
        scratch_shapes=[pltpu.VMEM(pair_features.shape, bf16), dma((share // fold,)), dma((share // fold,))],
        compiler_params=pltpu.CompilerParams(vmem_limit_bytes=VMEM_LIMIT),
        name="clip",
    )(raw, grads)


def solution(mesh):
    return jax.shard_map(
        functools.partial(shards, mesh.shape["slab"], mesh.shape["mode"]),
        mesh=mesh,
        in_specs=(
            P("slab", None, "mode"),
            P("slab"),
            P("mode"),
            P("slab", None),
            P(("slab", "mode"), None),
            P(),
            P(),
            P(),
        ),
        out_specs=(P(("slab", "mode"), None), P(), P(), P()),
        check_vma=False,
    )
```
